128 devices in a mesh: var: 16 (over y, z), own: 4 (over x), sub: 2 (over core).
Axes of the slice: x: 4, y: 4, z: 4, core: 2. Of those that a mesh axis runs over, the one named last changes fastest.
Arguments:
- capacity_blocks: bfloat16 [8192, 5, 128, 128], P(('var', 'own', 'sub')), may hold values from -0.0390625 to 0.0390625
- capacity_rows: int32 [8192, 5], P(('var', 'own', 'sub')), may hold values from 0 to 7, all different within a row
- cover_self: bfloat16 [8192, 128, 128], P(('var', 'own', 'sub')), may hold values from -0.5 to 0.5
- cover_prev: bfloat16 [8192, 128, 128], P(('var', 'own', 'sub')), may hold values from -0.5 to 0.5
- scaling: bfloat16 [8192, 128], P(('var', 'own', 'sub')), may hold values from 0.099609375 to 10
Outputs:
- cover_diag: bfloat16 [8192, 128, 128], P(('var', 'own', 'sub'))
- cover_lower: bfloat16 [8192, 128, 128], P(('var', 'own', 'sub'))
- capacity_normal: float32 [1024, 1024], P(('var', 'own', 'sub'))
The draws below stay inside these ranges and needn't reach their ends.
Inputs may be any that keep to these rules, and one draw needn't show every extreme that they name: `capacity_rows`: each column block names 5 different capacity row blocks, and every capacity row block is named somewhere.
All inputs are finite; a program needn't handle non-finite values.
Results may differ from the reference program's by a relative error of at most 0.0049.
Values may be sent and summed in bfloat16 or wider, within the bound.
A program may use at most 192 MiB of HBM per device.

```python
import math
import jax
import jax.numpy as jnp
from jax import lax

BLK = 128
NZ = 5
CAP = 8
CB_DEV = 64
NCB = 8192
DEVICES = 128


def steps_of(stream_key, dims, cuts, low, high):
    def one(axis_at, blocks):
        draws = jax.random.uniform(jax.random.fold_in(jax.random.fold_in(stream_key, 6), axis_at), (blocks,), jnp.float32, low / len(cuts), high / len(cuts))
        return jnp.repeat(jnp.exp(draws), dims[axis_at] // blocks).reshape((-1,) + (1,) * (len(dims) - axis_at - 1))

    loudness = one(*cuts[0])
    for cut in cuts[1:]:
        loudness = loudness * one(*cut)
    return loudness


def picks_of(stream_key, rows, count, top, lift):
    ranking = jax.random.permutation(jax.random.fold_in(stream_key, 1), count)
    pull = ranking
    for power in range(3):
        pull = pull * pull // count
    pull = pull * lift // count
    tickets = jax.random.randint(jax.random.fold_in(stream_key, 2), (rows, count), 0, 4096) + pull
    fixed_rows = jax.random.permutation(jax.random.fold_in(stream_key, 3), rows)[jnp.arange(count) % rows]
    tickets = jnp.where(jnp.arange(rows)[:, None] == fixed_rows[None, :], 1 << 14, tickets)
    merit = tickets * count + jnp.arange(count)
    return lax.top_k(merit.astype(jnp.int32), top)[1].astype(jnp.int32)


def scatter_about(own_key, dims, deviation, reach, shards=(), dtype=jnp.bfloat16):
    entries = jax.random.normal(own_key, dims, jnp.float32) * deviation
    if len(shards) > 0:
        entries = steps_of(own_key, dims, shards, -0.22, 0.18) * entries
    return jnp.clip(entries, min=-reach, max=reach).astype(dtype)


def setup_inputs(seed: int = 0) -> dict:
    splits = jax.random.split(jax.random.key(seed), 6)
    return {
        "capacity_blocks": scatter_about(splits[0], (NCB, NZ, BLK, BLK), (CB_DEV * DEVICES * NZ * BLK // (CAP * 32)) ** -0.5, 0.0390625, ((0, 128),)),
        "capacity_rows": picks_of(splits[1], NCB, CAP, NZ, 10240),
        "cover_self": scatter_about(splits[2], (NCB, BLK, BLK), BLK ** -0.5, 0.5, ((0, 128),)),
        "cover_prev": scatter_about(splits[3], (NCB, BLK, BLK), BLK ** -0.5, 0.5, ((0, 128),)),
        "scaling": jnp.clip(jnp.exp(math.log(10.0) - 4.609084 * jax.random.uniform(splits[4], (NCB, BLK), jnp.float32) ** steps_of(splits[4], (NCB, BLK), ((0, 128),), -0.2, 0.2)), 0.099609375, 10.0).astype(jnp.bfloat16),
    }


def accumulate(partial_value, inputs):
    blocks, row_ids, scale_row = inputs
    scaled = (blocks.astype(jnp.float32) * scale_row.astype(jnp.float32)[:, None, None, :]).astype(jnp.bfloat16)
    tile_sums = jnp.einsum("kpiv,kqjv->kpqij", scaled.astype(jnp.float32), blocks.astype(jnp.float32))
    per_block = row_ids.shape[1]
    left_rows = jnp.broadcast_to(row_ids[:, :, None], (row_ids.shape[0], per_block, per_block)).reshape(-1)
    right_rows = jnp.broadcast_to(row_ids[:, None, :], (row_ids.shape[0], per_block, per_block)).reshape(-1)
    edge_size = blocks.shape[-1]
    partial_value = partial_value.at[left_rows, :, right_rows, :].add(tile_sums.reshape(-1, edge_size, edge_size))
    return partial_value, None


def reference(capacity_blocks, capacity_rows, cover_self, cover_prev, scaling):
    total_blocks = capacity_blocks.shape[0]
    group_size = math.gcd(total_blocks, 64)
    turns = total_blocks // group_size
    inputs = (capacity_blocks.reshape((turns, group_size) + capacity_blocks.shape[1:]),
              capacity_rows.reshape(turns, group_size, -1),
              scaling.reshape(turns, group_size, -1))
    start = jnp.zeros((CAP, BLK, CAP, BLK), jnp.float32)
    result, unused = lax.scan(accumulate, start, inputs)
    capacity_normal = result.reshape(CAP * BLK, CAP * BLK)
    scaled_self = (cover_self.astype(jnp.float32) * scaling.astype(jnp.float32)[:, None, :]).astype(jnp.bfloat16)
    scale_prev = jnp.concatenate([jnp.zeros((1, BLK), jnp.bfloat16), scaling[:-1]], axis=0)
    self_prev = jnp.concatenate([jnp.zeros((1, BLK, BLK), jnp.bfloat16), cover_self[:-1]], axis=0)
    scaled_prev = (cover_prev.astype(jnp.float32) * scale_prev.astype(jnp.float32)[:, None, :]).astype(jnp.bfloat16)
    diag_sum = jnp.einsum("kiv,kjv->kij", scaled_self.astype(jnp.float32), cover_self.astype(jnp.float32))
    diag_sum = diag_sum + jnp.einsum("kiv,kjv->kij", scaled_prev.astype(jnp.float32), cover_prev.astype(jnp.float32))
    lower_sum = jnp.einsum("kiv,kjv->kij", scaled_prev.astype(jnp.float32), self_prev.astype(jnp.float32))
    return diag_sum.astype(jnp.bfloat16), lower_sum.astype(jnp.bfloat16), capacity_normal
```

```python
import functools

import jax
import jax.numpy as jnp
from jax import lax
from jax.experimental import pallas as pl
from jax.experimental.pallas import tpu as pltpu
from jax.sharding import PartitionSpec as P

MESH = pl.DeviceIdType.MESH
CAP = 8
TILE = 256
ORDER = (2, 1, 3, 0)
CHUNKS = 4
BATCHES = (
    ((0, 0), (0, 1), (0, 2), (0, 3), (1, 0), (2, 0), (3, 0)),
    ((1, 1), (1, 2), (1, 3), (2, 1), (3, 1)),
    ((2, 2), (2, 3), (3, 2)),
    ((3, 3),),
)
NT = (((1,), (1,)), ((), ()))


def kernel(sizes, cap_ref, rows_ref, self_ref, prev_ref, scal_ref, diag_ref, lower_ref, norm_ref, *scratch):
    local, per_block, edge = sizes
    group = local // CHUNKS
    scratch = list(scratch)
    raws = [scratch.pop(0) for _ in range(CHUNKS)]
    panels = [scratch.pop(0) for _ in range(CHUNKS)]
    core_send = [scratch.pop(0) for _ in range(4)]
    core_recv = [scratch.pop(0) for _ in range(4)]
    plane_send = [scratch.pop(0) for _ in range(4)]
    plane_recv = [scratch.pop(0) for _ in range(4)]
    (acc, root, dsc, cself, cprev, cdiag, clower, bnd_block, bnd_scale, ysum, yrecv, out_buf) = scratch[:12]
    (load_sem, cover_sem, out_sem, norm_sem, bnd_send, bnd_recv, core_ssem, core_rsem,
     plane_ssem, plane_rsem, y_ssem, y_rsem) = scratch[12:]

    var, own, sub = lax.axis_index("var"), lax.axis_index("own"), lax.axis_index("sub")
    y, z, x = var // 4, var % 4, own
    here = (var * 4 + own) * 2 + sub

    def device(index):
        return (index // 8, (index // 2) % 4, index % 2)

    after, before = device((here + 1) % 128), device((here + 127) % 128)
    other = (var, own, 1 - sub)

    def plane_peer(d):
        return (y * 4 + (z + d // 4) % 4, (x + d % 4) % 4, sub)

    def y_peer(t):
        return (((y + ORDER[t]) % 4) * 4 + z, x, sub)

    barrier = pltpu.get_barrier_semaphore()

    loads = []
    for c in range(CHUNKS):
        copy = pltpu.make_async_copy(
            cap_ref.at[pl.ds(c * group * per_block, group * per_block)],
            raws[c].at[pl.ds(0, group * per_block)],
            load_sem.at[c],
        )
        loads.append(copy)
    cover_loads = [
        pltpu.make_async_copy(self_ref, cself.at[pl.ds(1, local)], cover_sem.at[0]),
        pltpu.make_async_copy(prev_ref, cprev, cover_sem.at[1]),
    ]
    loads[0].start()
    loads[1].start()

    for peer in (other, after, before):
        pl.semaphore_signal(barrier, inc=1, device_id=peer, device_id_type=MESH)
    for t in range(3):
        pl.semaphore_signal(barrier, inc=1, device_id=y_peer(t), device_id_type=MESH)

    @pl.loop(1, 16)
    def _(d):
        pl.semaphore_signal(barrier, inc=1, device_id=plane_peer(d), device_id_type=MESH)

    for c in range(CHUNKS):
        raws[c][group * per_block] = jnp.zeros((edge, edge), jnp.bfloat16)
    scale = scal_ref[...].astype(jnp.float32)
    dsc[pl.ds(8, local), :] = scale
    root[...] = jnp.sqrt(scale)

    def build(c):
        @pl.loop(0, group)
        def _(kk):
            k = c * group + kk
            named = [rows_ref[k, p] for p in range(per_block)]
            d = root[pl.ds(k, 1), :]
            column = pl.ds(pl.multiple_of(kk * edge, edge), edge)
            for t in range(4):
                for h in range(2):
                    row = ((y + ORDER[t]) % 4) * 2 + h
                    at = jnp.int32(group * per_block)
                    for p in range(per_block):
                        at = jnp.where(named[p] == row, kk * per_block + p, at)
                    block = raws[c][at]
                    panels[c][pl.ds((t * 2 + h) * edge, edge), column] = (
                        block.astype(jnp.float32) * d
                    ).astype(jnp.bfloat16)

    def product(c, t, j):
        part = lax.dot_general(
            panels[c][pl.ds(t * TILE, TILE), :],
            panels[c][pl.ds(j * TILE, TILE), :],
            NT,
            preferred_element_type=jnp.float32,
        )
        unit = (pl.ds(t * TILE, TILE), pl.ds(j * TILE, TILE))
        if c == 0:
            acc[unit] = part
        else:
            acc[unit] += part

    def unit_of(t, j):
        for c in range(CHUNKS):
            product(c, t, j)

    core_copies = [
        pltpu.make_async_remote_copy(
            src_ref=core_send[b].at[1 - sub],
            dst_ref=core_recv[b],
            send_sem=core_ssem.at[b],
            recv_sem=core_rsem.at[b],
            device_id=other,
            device_id_type=MESH,
        )
        for b in range(4)
    ]

    def pack(b):
        for u, (t, j) in enumerate(BATCHES[b]):
            if t <= j:
                value = acc[pl.ds(t * TILE, TILE), pl.ds(j * TILE, TILE)]
            else:
                value = acc[pl.ds(j * TILE, TILE), pl.ds(t * TILE, TILE)].T
            value = value.reshape(16, 2, 8, TILE).astype(jnp.bfloat16)
            for c in range(2):
                core_send[b][c, :, pl.ds(u * 8, 8), :] = value[:, c]
        core_copies[b].start()

    def plane_copy(b, d):
        to = ((z + d // 4) % 4) * 4 + (x + d % 4) % 4
        return pltpu.make_async_remote_copy(
            src_ref=plane_send[b].at[to],
            dst_ref=plane_recv[b].at[d],
            send_sem=plane_ssem.at[b, d],
            recv_sem=plane_rsem.at[b, d],
            device_id=plane_peer(d),
            device_id_type=MESH,
        )

    def add_core(b):
        core_copies[b].wait_recv()
        plane_send[b][...] = (
            core_send[b][sub].astype(jnp.float32) + core_recv[b][...].astype(jnp.float32)
        ).astype(jnp.bfloat16)

        @pl.loop(1, 16)
        def _(d):
            plane_copy(b, d).start()

    y_copies = [
        pltpu.make_async_remote_copy(
            src_ref=ysum.at[t],
            dst_ref=yrecv.at[t],
            send_sem=y_ssem.at[t],
            recv_sem=y_rsem.at[t],
            device_id=y_peer(t),
            device_id_type=MESH,
        )
        for t in range(3)
    ]

    def add_plane(b):
        @pl.loop(1, 16)
        def _(d):
            plane_copy(b, d).wait_recv()

        total = plane_send[b][z * 4 + x].astype(jnp.float32)
        for d in range(1, 16):
            total = total + plane_recv[b][d].astype(jnp.float32)
        for u, (t, j) in enumerate(BATCHES[b]):
            column = pl.multiple_of(((y + ORDER[j]) % 4) * TILE, TILE)
            ysum[t, :, pl.ds(column, TILE)] = total[u * 8 : (u + 1) * 8]
        if b < 3:
            y_copies[b].start()

    def cover(c):
        @pl.loop(c * group, (c + 1) * group)
        def _(k):
            d = dsc[pl.ds(k + 8, 1), :].astype(jnp.bfloat16)
            d_prev = dsc[pl.ds(k + 7, 1), :].astype(jnp.bfloat16)
            block, link = cself[k + 1], cprev[k]
            scaled, scaled_link = block * d, link * d_prev
            total = lax.dot_general(
                jnp.concatenate([scaled, scaled_link], axis=1),
                jnp.concatenate([block, link], axis=1),
                NT,
                preferred_element_type=jnp.float32,
            )
            cdiag[k] = total.astype(jnp.bfloat16)
            clower[k] = lax.dot_general(
                scaled_link, cself[k], NT, preferred_element_type=jnp.float32
            ).astype(jnp.bfloat16)

        part = pl.ds(c * group, group)
        copies = [
            pltpu.make_async_copy(cdiag.at[part], diag_ref.at[part], out_sem.at[0, c]),
            pltpu.make_async_copy(clower.at[part], lower_ref.at[part], out_sem.at[1, c]),
        ]
        for copy in copies:
            copy.start()
        return copies

    for c in range(CHUNKS):
        loads[c].wait()
        if c + 2 < CHUNKS:
            loads[c + 2].start()
        elif c + 2 == CHUNKS:
            cover_loads[0].start()
            cover_loads[1].start()
        build(c)
        for j in range(4):
            product(c, 0, j)

    pl.semaphore_wait(barrier, 21)
    boundary = [
        pltpu.make_async_remote_copy(
            src_ref=self_ref.at[local - 1],
            dst_ref=bnd_block,
            send_sem=bnd_send.at[0],
            recv_sem=bnd_recv.at[0],
            device_id=after,
            device_id_type=MESH,
        ),
        pltpu.make_async_remote_copy(
            src_ref=scal_ref.at[pl.ds(local - 16, 16)],
            dst_ref=bnd_scale,
            send_sem=bnd_send.at[1],
            recv_sem=bnd_recv.at[1],
            device_id=after,
            device_id_type=MESH,
        ),
    ]
    for copy in boundary:
        copy.start()
    pack(0)
    unit_of(1, 1)
    add_core(0)
    unit_of(1, 2)
    unit_of(1, 3)
    pack(1)
    unit_of(2, 2)
    add_core(1)
    unit_of(2, 3)
    pack(2)
    unit_of(3, 3)
    pack(3)
    add_core(2)

    for copy in cover_loads:
        copy.wait()
    for copy in boundary:
        copy.wait_recv()
    first = here == 0
    cself[0] = jnp.where(first, jnp.zeros_like(bnd_block), bnd_block[...])
    dsc[pl.ds(7, 1), :] = jnp.where(first, 0.0, bnd_scale[...].astype(jnp.float32)[15:16, :])

    outs = []
    outs += cover(0)
    add_core(3)
    add_plane(0)
    outs += cover(1)
    add_plane(1)
    outs += cover(2)
    add_plane(2)
    outs += cover(3)
    add_plane(3)
    total = ysum[3]
    for t in range(3):
        y_copies[t].wait_recv()
        total = total + yrecv[t]
    out_buf[...] = total
    last = pltpu.make_async_copy(out_buf, norm_ref, norm_sem)
    last.start()
    for copy in boundary + core_copies + y_copies:
        copy.wait_send()
    for b in range(4):
        @pl.loop(1, 16)
        def _(d):
            plane_copy(b, d).wait_send()
    for copy in outs:
        copy.wait()
    last.wait()


def body(capacity_blocks, capacity_rows, cover_self, cover_prev, scaling):
    local, per_block, edge, _ = capacity_blocks.shape
    group = local // CHUNKS
    full = CAP * edge
    bf16, f32 = jnp.bfloat16, jnp.float32
    counts = [len(batch) for batch in BATCHES]
    dma = pltpu.SemaphoreType.DMA
    scratch = [pltpu.VMEM((group * per_block + 1, edge, edge), bf16) for _ in range(CHUNKS)]
    scratch += [pltpu.VMEM((full, group * edge), bf16) for _ in range(CHUNKS)]
    scratch += [pltpu.VMEM((2, 16, n * 8, TILE), bf16) for n in counts]
    scratch += [pltpu.VMEM((16, n * 8, TILE), bf16) for n in counts]
    scratch += [pltpu.VMEM((16, n * 8, TILE), bf16) for n in counts]
    scratch += [pltpu.VMEM((16, n * 8, TILE), bf16) for n in counts]
    scratch += [
        pltpu.VMEM((full, full), f32),
        pltpu.VMEM((local, edge), f32),
        pltpu.VMEM((local + 8, edge), f32),
        pltpu.VMEM((local + 1, edge, edge), bf16),
        pltpu.VMEM((local, edge, edge), bf16),
        pltpu.VMEM((local, edge, edge), bf16),
        pltpu.VMEM((local, edge, edge), bf16),
        pltpu.VMEM((edge, edge), bf16),
        pltpu.VMEM((16, edge), bf16),
        pltpu.VMEM((4, 8, full), f32),
        pltpu.VMEM((3, 8, full), f32),
        pltpu.VMEM((8, full), f32),
    ]
    scratch += [
        dma((CHUNKS,)), dma((2,)), dma((2, CHUNKS)), dma(()), dma((2,)), dma((2,)),
        dma((4,)), dma((4,)), dma((4, 16)), dma((4, 16)), dma((3,)), dma((3,)),
    ]
    anywhere = pl.BlockSpec(memory_space=pl.ANY)
    return pl.pallas_call(
        functools.partial(kernel, (local, per_block, edge)),
        out_shape=(
            jax.ShapeDtypeStruct((local, edge, edge), bf16),
            jax.ShapeDtypeStruct((local, edge, edge), bf16),
            jax.ShapeDtypeStruct((8, full), f32),
        ),
        in_specs=[
            anywhere,
            pl.BlockSpec(memory_space=pltpu.SMEM),
            anywhere,
            anywhere,
            pl.BlockSpec(memory_space=pltpu.VMEM),
        ],
        out_specs=(anywhere, anywhere, anywhere),
        scratch_shapes=scratch,
        compiler_params=pltpu.CompilerParams(
            collective_id=0, has_side_effects=True, vmem_limit_bytes=60 << 20
        ),
    )(capacity_blocks.reshape(local * per_block, edge, edge), capacity_rows, cover_self, cover_prev, scaling)


def solution(mesh):
    axes = ("var", "own", "sub")
    placed = (P(axes, None, None, None), P(axes, None), P(axes, None, None), P(axes, None, None), P(axes, None))
    return jax.shard_map(
        body,
        mesh=mesh,
        in_specs=placed,
        out_specs=(P(axes, None, None), P(axes, None, None), P(axes, None)),
        check_vma=False,
    )
```

```python
import functools

import jax
import jax.numpy as jnp
from jax import lax
from jax.experimental import pallas as pl
from jax.experimental.pallas import tpu as pltpu
from jax.sharding import PartitionSpec as P

MESH = pl.DeviceIdType.MESH
CAP = 8
TILE = 256
ORDER = (2, 1, 3, 0)
CHUNKS = (8, 16, 20, 20)
STARTS = (0, 8, 24, 44)
BATCHES = (
    ((0, 0), (0, 1), (0, 2), (0, 3), (1, 0), (2, 0), (3, 0)),
    ((1, 1), (1, 2), (1, 3), (2, 1), (3, 1)),
    ((2, 2), (2, 3), (3, 2)),
    ((3, 3),),
)
NT = (((1,), (1,)), ((), ()))


def kernel(sizes, cap_ref, rows_ref, self_ref, prev_ref, scal_ref, diag_ref, lower_ref, norm_ref, *scratch):
    local, per_block, edge = sizes
    group = local // 4
    scratch = list(scratch)
    raws = [scratch.pop(0) for _ in CHUNKS]
    scaled_raws = [scratch.pop(0) for _ in CHUNKS]
    core_send = [scratch.pop(0) for _ in range(4)]
    core_recv = [scratch.pop(0) for _ in range(4)]
    plane_send = [scratch.pop(0) for _ in range(4)]
    plane_recv = [scratch.pop(0) for _ in range(4)]
    (acc, dsc, cself, cprev, bnd_block, bnd_scale, ysum, yrecv) = scratch[:8]
    (load_sem, cover_sem, bnd_send, bnd_recv, core_ssem, core_rsem,
     plane_ssem, plane_rsem, y_ssem, y_rsem) = scratch[8:]

    var, own, sub = lax.axis_index("var"), lax.axis_index("own"), lax.axis_index("sub")
    y, z, x = var // 4, var % 4, own
    here = (var * 4 + own) * 2 + sub

    def device(index):
        return (index // 8, (index // 2) % 4, index % 2)

    after, before = device((here + 1) % 128), device((here + 127) % 128)
    other = (var, own, 1 - sub)

    def plane_peer(d):
        return (y * 4 + (z + d // 4) % 4, (x + d % 4) % 4, sub)

    def y_peer(t):
        return (((y + ORDER[t]) % 4) * 4 + z, x, sub)

    barrier = pltpu.get_barrier_semaphore()

    loads = []
    for c, size in enumerate(CHUNKS):
        copy = pltpu.make_async_copy(
            cap_ref.at[pl.ds(STARTS[c] * per_block, size * per_block)],
            raws[c].at[pl.ds(0, size * per_block)],
            load_sem.at[c],
        )
        loads.append(copy)
    cover_loads = [
        pltpu.make_async_copy(self_ref, cself.at[pl.ds(1, local)], cover_sem.at[0]),
        pltpu.make_async_copy(prev_ref, cprev, cover_sem.at[1]),
    ]
    for copy in loads:
        copy.start()

    for peer in (other, after, before):
        pl.semaphore_signal(barrier, inc=1, device_id=peer, device_id_type=MESH)
    for t in range(3):
        pl.semaphore_signal(barrier, inc=1, device_id=y_peer(t), device_id_type=MESH)

    @pl.loop(1, 16)
    def _(d):
        pl.semaphore_signal(barrier, inc=1, device_id=plane_peer(d), device_id_type=MESH)

    blank = jnp.zeros((edge, edge), jnp.bfloat16)
    for c, size in enumerate(CHUNKS):
        raws[c][size * per_block] = blank
        scaled_raws[c][size * per_block] = blank
    dsc[pl.ds(8, local), :] = scal_ref[...].astype(jnp.float32)

    places = {}

    def place(c):
        for kk in range(CHUNKS[c]):
            named = [rows_ref[p, STARTS[c] + kk] for p in range(per_block)]
            for t in range(4):
                for h in range(2):
                    row = ((y + ORDER[t]) % 4) * 2 + h
                    at = jnp.int32(CHUNKS[c] * per_block)
                    for p in range(per_block):
                        at = jnp.where(named[p] == row, kk * per_block + p, at)
                    places[c, kk, t, h] = at

    def apply_scale(c):
        for kk in range(CHUNKS[c]):
            d = dsc[pl.ds(8 + STARTS[c] + kk, 1), :].astype(jnp.bfloat16)
            for p in range(per_block):
                scaled_raws[c][kk * per_block + p] = raws[c][kk * per_block + p] * d

    def operand(source, c, t):
        halves = [
            jnp.concatenate([source[c][places[c, kk, t, h]] for kk in range(CHUNKS[c])], axis=1)
            for h in range(2)
        ]
        return jnp.concatenate(halves, axis=0)

    def product(c, t, j):
        part = lax.dot_general(
            operand(scaled_raws, c, t), operand(raws, c, j), NT, preferred_element_type=jnp.float32
        )
        unit = (pl.ds(t * TILE, TILE), pl.ds(j * TILE, TILE))
        if c == 0:
            acc[unit] = part
        else:
            acc[unit] += part

    def unit_of(t, j):
        for c in range(len(CHUNKS)):
            product(c, t, j)

    core_copies = [
        pltpu.make_async_remote_copy(
            src_ref=core_send[b].at[1 - sub],
            dst_ref=core_recv[b],
            send_sem=core_ssem.at[b],
            recv_sem=core_rsem.at[b],
            device_id=other,
            device_id_type=MESH,
        )
        for b in range(4)
    ]

    def pack(b):
        for u, (t, j) in enumerate(BATCHES[b]):
            if t <= j:
                value = acc[pl.ds(t * TILE, TILE), pl.ds(j * TILE, TILE)]
            else:
                value = acc[pl.ds(j * TILE, TILE), pl.ds(t * TILE, TILE)].T
            value = value.reshape(16, 2, 8, TILE).astype(jnp.bfloat16)
            for c in range(2):
                core_send[b][c, :, pl.ds(u * 8, 8), :] = value[:, c]
        core_copies[b].start()

    def plane_copy(b, d):
        to = ((z + d // 4) % 4) * 4 + (x + d % 4) % 4
        return pltpu.make_async_remote_copy(
            src_ref=plane_send[b].at[to],
            dst_ref=plane_recv[b].at[d],
            send_sem=plane_ssem.at[b, d],
            recv_sem=plane_rsem.at[b, d],
            device_id=plane_peer(d),
            device_id_type=MESH,
        )

    def add_core(b):
        core_copies[b].wait_recv()
        plane_send[b][...] = (
            core_send[b][sub].astype(jnp.float32) + core_recv[b][...].astype(jnp.float32)
        ).astype(jnp.bfloat16)

        @pl.loop(1, 16)
        def _(d):
            plane_copy(b, d).start()

    y_copies = [
        pltpu.make_async_remote_copy(
            src_ref=ysum.at[t],
            dst_ref=yrecv.at[t],
            send_sem=y_ssem.at[t],
            recv_sem=y_rsem.at[t],
            device_id=y_peer(t),
            device_id_type=MESH,
        )
        for t in range(3)
    ]

    def add_plane(b):
        @pl.loop(1, 16)
        def _(d):
            plane_copy(b, d).wait_recv()

        total = plane_send[b][z * 4 + x].astype(jnp.float32)
        for d in range(1, 16):
            total = total + plane_recv[b][d].astype(jnp.float32)
        for u, (t, j) in enumerate(BATCHES[b]):
            column = pl.multiple_of(((y + ORDER[j]) % 4) * TILE, TILE)
            ysum[t, :, pl.ds(column, TILE)] = total[u * 8 : (u + 1) * 8]
        if b < 3:
            y_copies[b].start()

    def cover(c):
        @pl.loop(c * group, (c + 1) * group, unroll=group)
        def _(k):
            d = dsc[pl.ds(k + 8, 1), :].astype(jnp.bfloat16)
            d_prev = dsc[pl.ds(k + 7, 1), :].astype(jnp.bfloat16)
            block, link = cself[k + 1], cprev[k]
            scaled, scaled_link = block * d, link * d_prev
            total = lax.dot_general(
                jnp.concatenate([scaled, scaled_link], axis=1),
                jnp.concatenate([block, link], axis=1),
                NT,
                preferred_element_type=jnp.float32,
            )
            diag_ref[k] = total.astype(jnp.bfloat16)
            lower_ref[k] = lax.dot_general(
                scaled_link, cself[k], NT, preferred_element_type=jnp.float32
            ).astype(jnp.bfloat16)

    for copy in cover_loads:
        copy.start()
    for c in range(len(CHUNKS)):
        place(c)
        loads[c].wait()
        apply_scale(c)
        for j in range(4):
            product(c, 0, j)

    pl.semaphore_wait(barrier, 21)
    boundary = [
        pltpu.make_async_remote_copy(
            src_ref=self_ref.at[local - 1],
            dst_ref=bnd_block,
            send_sem=bnd_send.at[0],
            recv_sem=bnd_recv.at[0],
            device_id=after,
            device_id_type=MESH,
        ),
        pltpu.make_async_remote_copy(
            src_ref=scal_ref.at[pl.ds(local - 16, 16)],
            dst_ref=bnd_scale,
            send_sem=bnd_send.at[1],
            recv_sem=bnd_recv.at[1],
            device_id=after,
            device_id_type=MESH,
        ),
    ]
    for copy in boundary:
        copy.start()
    pack(0)
    unit_of(1, 1)
    add_core(0)
    unit_of(1, 2)
    unit_of(1, 3)
    pack(1)
    unit_of(2, 2)
    add_core(1)
    unit_of(2, 3)
    pack(2)
    unit_of(3, 3)
    pack(3)
    add_core(2)

    for copy in cover_loads:
        copy.wait()
    for copy in boundary:
        copy.wait_recv()
    first = here == 0
    cself[0] = jnp.where(first, jnp.zeros_like(bnd_block), bnd_block[...])
    dsc[pl.ds(7, 1), :] = jnp.where(first, 0.0, bnd_scale[...].astype(jnp.float32)[15:16, :])

    cover(0)
    add_core(3)
    add_plane(0)
    cover(1)
    add_plane(1)
    cover(2)
    add_plane(2)
    cover(3)
    add_plane(3)
    total = ysum[3]
    for t in range(3):
        y_copies[t].wait_recv()
        total = total + yrecv[t]
    norm_ref[...] = total
    for copy in boundary + core_copies + y_copies:
        copy.wait_send()
    for b in range(4):
        @pl.loop(1, 16)
        def _(d):
            plane_copy(b, d).wait_send()


def body(capacity_blocks, capacity_rows, cover_self, cover_prev, scaling):
    local, per_block, edge, _ = capacity_blocks.shape
    full = CAP * edge
    bf16, f32 = jnp.bfloat16, jnp.float32
    counts = [len(batch) for batch in BATCHES]
    dma = pltpu.SemaphoreType.DMA
    scratch = [pltpu.VMEM((n * per_block + 1, edge, edge), bf16) for n in CHUNKS * 2]
    scratch += [pltpu.VMEM((2, 16, n * 8, TILE), bf16) for n in counts]
    scratch += [pltpu.VMEM((16, n * 8, TILE), bf16) for n in counts]
    scratch += [pltpu.VMEM((16, n * 8, TILE), bf16) for n in counts]
    scratch += [pltpu.VMEM((16, n * 8, TILE), bf16) for n in counts]
    scratch += [
        pltpu.VMEM((full, full), f32),
        pltpu.VMEM((local + 8, edge), f32),
        pltpu.VMEM((local + 1, edge, edge), bf16),
        pltpu.VMEM((local, edge, edge), bf16),
        pltpu.VMEM((edge, edge), bf16),
        pltpu.VMEM((16, edge), bf16),
        pltpu.VMEM((4, 8, full), f32),
        pltpu.VMEM((3, 8, full), f32),
    ]
    scratch += [
        dma((len(CHUNKS),)), dma((2,)), dma((2,)), dma((2,)),
        dma((4,)), dma((4,)), dma((4, 16)), dma((4, 16)), dma((3,)), dma((3,)),
    ]
    anywhere = pl.BlockSpec(memory_space=pl.ANY)
    return pl.pallas_call(
        functools.partial(kernel, (local, per_block, edge)),
        out_shape=(
            pltpu.VMEM((local, edge, edge), bf16),
            pltpu.VMEM((local, edge, edge), bf16),
            pltpu.VMEM((8, full), f32),
        ),
        in_specs=[
            anywhere,
            pl.BlockSpec(memory_space=pltpu.SMEM),
            anywhere,
            anywhere,
            pl.BlockSpec(memory_space=pltpu.VMEM),
        ],
        out_specs=(pl.BlockSpec(memory_space=pltpu.VMEM),) * 3,
        scratch_shapes=scratch,
        compiler_params=pltpu.CompilerParams(
            collective_id=0, has_side_effects=True, vmem_limit_bytes=50 << 20
        ),
    )(capacity_blocks.reshape(local * per_block, edge, edge), capacity_rows.T, cover_self, cover_prev, scaling)


def solution(mesh):
    axes = ("var", "own", "sub")
    placed = (P(axes, None, None, None), P(axes, None), P(axes, None, None), P(axes, None, None), P(axes, None))
    return jax.shard_map(
        body,
        mesh=mesh,
        in_specs=placed,
        out_specs=(P(axes, None, None), P(axes, None, None), P(axes, None)),
        check_vma=False,
    )
```

```python
import functools

import jax
import jax.numpy as jnp
from jax import lax
from jax.experimental import pallas as pl
from jax.experimental.pallas import tpu as pltpu
from jax.sharding import PartitionSpec as P

MESH = pl.DeviceIdType.MESH
CAP = 8
TILE = 256
ORDER = (2, 1, 3, 0)
CHUNKS = (8, 16, 20, 20)
STARTS = (0, 8, 24, 44)
BATCHES = (
    ((0, 0), (0, 1), (0, 2), (0, 3), (1, 0), (2, 0), (3, 0)),
    ((1, 1), (1, 2), (1, 3), (2, 1), (3, 1)),
    ((2, 2), (2, 3), (3, 2)),
    ((3, 3),),
)
NT = (((1,), (1,)), ((), ()))


def kernel(sizes, cap_ref, rows_ref, self_ref, prev_ref, scal_ref, diag_ref, lower_ref, norm_ref, *scratch):
    local, per_block, edge = sizes
    group = local // 4
    scratch = list(scratch)
    raws = [scratch.pop(0) for _ in CHUNKS]
    scaled_raws = [scratch.pop(0) for _ in CHUNKS]
    core_send = [scratch.pop(0) for _ in range(4)]
    core_recv = [scratch.pop(0) for _ in range(4)]
    first_send = [scratch.pop(0) for _ in range(4)]
    first_recv = [scratch.pop(0) for _ in range(4)]
    second_send = [scratch.pop(0) for _ in range(4)]
    second_recv = [scratch.pop(0) for _ in range(4)]
    (acc, dsc, cself, cprev, bnd_block, bnd_scale, ysum, yrecv) = scratch[:8]
    (load_sem, cover_sem, bnd_send, bnd_recv, core_ssem, core_rsem,
     first_ssem, first_rsem, second_ssem, second_rsem, y_ssem, y_rsem) = scratch[8:]

    var, own, sub = lax.axis_index("var"), lax.axis_index("own"), lax.axis_index("sub")
    y, z, x = var // 4, var % 4, own
    here = (var * 4 + own) * 2 + sub

    def device(index):
        return (index // 8, (index // 2) % 4, index % 2)

    after, before = device((here + 1) % 128), device((here + 127) % 128)
    other = (var, own, 1 - sub)

    my_first, my_second = z * (1 - sub) + x * sub, x * (1 - sub) + z * sub

    def first_peer(d):
        return (y * 4 + (z + d * (1 - sub)) % 4, (x + d * sub) % 4, sub)

    def second_peer(d):
        return (y * 4 + (z + d * sub) % 4, (x + d * (1 - sub)) % 4, sub)

    def y_peer(t):
        return (((y + ORDER[t]) % 4) * 4 + z, x, sub)

    barrier = pltpu.get_barrier_semaphore()

    loads = []
    for c, size in enumerate(CHUNKS):
        copy = pltpu.make_async_copy(
            cap_ref.at[pl.ds(STARTS[c] * per_block, size * per_block)],
            raws[c].at[pl.ds(0, size * per_block)],
            load_sem.at[c],
        )
        loads.append(copy)
    cover_loads = [
        pltpu.make_async_copy(self_ref, cself.at[pl.ds(1, local)], cover_sem.at[0]),
        pltpu.make_async_copy(prev_ref, cprev, cover_sem.at[1]),
    ]
    for copy in loads:
        copy.start()

    for peer in (other, after, before):
        pl.semaphore_signal(barrier, inc=1, device_id=peer, device_id_type=MESH)
    for t in range(3):
        pl.semaphore_signal(barrier, inc=1, device_id=y_peer(t), device_id_type=MESH)

    for d in range(1, 4):
        pl.semaphore_signal(barrier, inc=1, device_id=first_peer(d), device_id_type=MESH)
        pl.semaphore_signal(barrier, inc=1, device_id=second_peer(d), device_id_type=MESH)

    blank = jnp.zeros((edge, edge), jnp.bfloat16)
    for c, size in enumerate(CHUNKS):
        raws[c][size * per_block] = blank
        scaled_raws[c][size * per_block] = blank
    dsc[pl.ds(8, local), :] = scal_ref[...].astype(jnp.float32)

    places = {}

    def place(c):
        for kk in range(CHUNKS[c]):
            named = [rows_ref[p, STARTS[c] + kk] for p in range(per_block)]
            for t in range(4):
                for h in range(2):
                    row = ((y + ORDER[t]) % 4) * 2 + h
                    at = jnp.int32(CHUNKS[c] * per_block)
                    for p in range(per_block):
                        at = jnp.where(named[p] == row, kk * per_block + p, at)
                    places[c, kk, t, h] = at

    def apply_scale(c):
        for kk in range(CHUNKS[c]):
            d = dsc[pl.ds(8 + STARTS[c] + kk, 1), :].astype(jnp.bfloat16)
            for p in range(per_block):
                scaled_raws[c][kk * per_block + p] = raws[c][kk * per_block + p] * d

    def operand(source, c, t):
        halves = [
            jnp.concatenate([source[c][places[c, kk, t, h]] for kk in range(CHUNKS[c])], axis=1)
            for h in range(2)
        ]
        return jnp.concatenate(halves, axis=0)

    def product(c, t, j):
        part = lax.dot_general(
            operand(scaled_raws, c, t), operand(raws, c, j), NT, preferred_element_type=jnp.float32
        )
        unit = (pl.ds(t * TILE, TILE), pl.ds(j * TILE, TILE))
        if c == 0:
            acc[unit] = part
        else:
            acc[unit] += part

    def unit_of(t, j):
        for c in range(len(CHUNKS)):
            product(c, t, j)

    core_copies = [
        pltpu.make_async_remote_copy(
            src_ref=core_send[b].at[1 - sub],
            dst_ref=core_recv[b],
            send_sem=core_ssem.at[b],
            recv_sem=core_rsem.at[b],
            device_id=other,
            device_id_type=MESH,
        )
        for b in range(4)
    ]

    def pack(b):
        for u, (t, j) in enumerate(BATCHES[b]):
            if t <= j:
                value = acc[pl.ds(t * TILE, TILE), pl.ds(j * TILE, TILE)]
            else:
                value = acc[pl.ds(j * TILE, TILE), pl.ds(t * TILE, TILE)].T
            value = value.reshape(16, 2, 8, TILE).astype(jnp.bfloat16)
            for c in range(2):
                core_send[b][c, :, pl.ds(u * 8, 8), :] = value[:, c]
        core_copies[b].start()

    first_copies = [
        [
            pltpu.make_async_remote_copy(
                src_ref=first_send[b].at[(my_first + d) % 4],
                dst_ref=first_recv[b].at[d],
                send_sem=first_ssem.at[b, d],
                recv_sem=first_rsem.at[b, d],
                device_id=first_peer(d),
                device_id_type=MESH,
            )
            for d in range(1, 4)
        ]
        for b in range(4)
    ]
    second_copies = [
        [
            pltpu.make_async_remote_copy(
                src_ref=second_send[b].at[(my_second + d) % 4],
                dst_ref=second_recv[b].at[d],
                send_sem=second_ssem.at[b, d],
                recv_sem=second_rsem.at[b, d],
                device_id=second_peer(d),
                device_id_type=MESH,
            )
            for d in range(1, 4)
        ]
        for b in range(4)
    ]

    def add_core(b):
        core_copies[b].wait_recv()
        for f in range(4):
            for g in range(4):
                at = (f * 4 + g) * (1 - sub) + (g * 4 + f) * sub
                first_send[b][f, g] = (
                    core_send[b][sub, at].astype(jnp.float32) + core_recv[b][at].astype(jnp.float32)
                ).astype(jnp.bfloat16)
        for copy in first_copies[b]:
            copy.start()

    def add_first(b):
        for copy in first_copies[b]:
            copy.wait_recv()
        total = first_send[b][my_first].astype(jnp.float32)
        for d in range(1, 4):
            total = total + first_recv[b][d].astype(jnp.float32)
        second_send[b][...] = total.astype(jnp.bfloat16)
        for copy in second_copies[b]:
            copy.start()

    y_copies = [
        pltpu.make_async_remote_copy(
            src_ref=ysum.at[t],
            dst_ref=yrecv.at[t],
            send_sem=y_ssem.at[t],
            recv_sem=y_rsem.at[t],
            device_id=y_peer(t),
            device_id_type=MESH,
        )
        for t in range(3)
    ]

    def add_second(b):
        for copy in second_copies[b]:
            copy.wait_recv()
        total = second_send[b][my_second].astype(jnp.float32)
        for d in range(1, 4):
            total = total + second_recv[b][d].astype(jnp.float32)
        for u, (t, j) in enumerate(BATCHES[b]):
            column = pl.multiple_of(((y + ORDER[j]) % 4) * TILE, TILE)
            ysum[t, :, pl.ds(column, TILE)] = total[u * 8 : (u + 1) * 8]
        if b < 3:
            y_copies[b].start()

    def cover(c):
        @pl.loop(c * group, (c + 1) * group, unroll=group)
        def _(k):
            d = dsc[pl.ds(k + 8, 1), :].astype(jnp.bfloat16)
            d_prev = dsc[pl.ds(k + 7, 1), :].astype(jnp.bfloat16)
            block, link = cself[k + 1], cprev[k]
            scaled, scaled_link = block * d, link * d_prev
            total = lax.dot_general(
                jnp.concatenate([scaled, scaled_link], axis=1),
                jnp.concatenate([block, link], axis=1),
                NT,
                preferred_element_type=jnp.float32,
            )
            diag_ref[k] = total.astype(jnp.bfloat16)
            lower_ref[k] = lax.dot_general(
                scaled_link, cself[k], NT, preferred_element_type=jnp.float32
            ).astype(jnp.bfloat16)

    for copy in cover_loads:
        copy.start()
    for c in range(len(CHUNKS)):
        place(c)
        loads[c].wait()
        apply_scale(c)
        for j in range(4):
            product(c, 0, j)

    pl.semaphore_wait(barrier, 12)
    boundary = [
        pltpu.make_async_remote_copy(
            src_ref=self_ref.at[local - 1],
            dst_ref=bnd_block,
            send_sem=bnd_send.at[0],
            recv_sem=bnd_recv.at[0],
            device_id=after,
            device_id_type=MESH,
        ),
        pltpu.make_async_remote_copy(
            src_ref=scal_ref.at[pl.ds(local - 16, 16)],
            dst_ref=bnd_scale,
            send_sem=bnd_send.at[1],
            recv_sem=bnd_recv.at[1],
            device_id=after,
            device_id_type=MESH,
        ),
    ]
    for copy in boundary:
        copy.start()
    pack(0)
    unit_of(1, 1)
    unit_of(1, 2)
    add_core(0)
    unit_of(1, 3)
    pack(1)
    unit_of(2, 2)
    unit_of(2, 3)
    add_core(1)
    pack(2)
    unit_of(3, 3)
    pack(3)
    add_core(2)

    for copy in cover_loads:
        copy.wait()
    for copy in boundary:
        copy.wait_recv()
    first = here == 0
    cself[0] = jnp.where(first, jnp.zeros_like(bnd_block), bnd_block[...])
    dsc[pl.ds(7, 1), :] = jnp.where(first, 0.0, bnd_scale[...].astype(jnp.float32)[15:16, :])

    cover(0)
    add_core(3)
    add_first(0)
    cover(1)
    add_first(1)
    add_second(0)
    cover(2)
    add_first(2)
    add_second(1)
    cover(3)
    add_first(3)
    add_second(2)
    add_second(3)
    total = ysum[3]
    for t in range(3):
        y_copies[t].wait_recv()
        total = total + yrecv[t]
    norm_ref[...] = total
    for copy in boundary + core_copies + y_copies:
        copy.wait_send()
    for b in range(4):
        for copy in first_copies[b] + second_copies[b]:
            copy.wait_send()


def body(capacity_blocks, capacity_rows, cover_self, cover_prev, scaling):
    local, per_block, edge, _ = capacity_blocks.shape
    full = CAP * edge
    bf16, f32 = jnp.bfloat16, jnp.float32
    counts = [len(batch) for batch in BATCHES]
    dma = pltpu.SemaphoreType.DMA
    scratch = [pltpu.VMEM((n * per_block + 1, edge, edge), bf16) for n in CHUNKS * 2]
    scratch += [pltpu.VMEM((2, 16, n * 8, TILE), bf16) for n in counts]
    scratch += [pltpu.VMEM((16, n * 8, TILE), bf16) for n in counts]
    scratch += [pltpu.VMEM((4, 4, n * 8, TILE), bf16) for n in counts * 2]
    scratch += [pltpu.VMEM((4, n * 8, TILE), bf16) for n in counts * 2]
    scratch += [
        pltpu.VMEM((full, full), f32),
        pltpu.VMEM((local + 8, edge), f32),
        pltpu.VMEM((local + 1, edge, edge), bf16),
        pltpu.VMEM((local, edge, edge), bf16),
        pltpu.VMEM((edge, edge), bf16),
        pltpu.VMEM((16, edge), bf16),
        pltpu.VMEM((4, 8, full), f32),
        pltpu.VMEM((3, 8, full), f32),
    ]
    scratch += [
        dma((len(CHUNKS),)), dma((2,)), dma((2,)), dma((2,)),
        dma((4,)), dma((4,)), dma((4, 4)), dma((4, 4)), dma((4, 4)), dma((4, 4)), dma((3,)), dma((3,)),
    ]
    anywhere = pl.BlockSpec(memory_space=pl.ANY)
    return pl.pallas_call(
        functools.partial(kernel, (local, per_block, edge)),
        out_shape=(
            pltpu.VMEM((local, edge, edge), bf16),
            pltpu.VMEM((local, edge, edge), bf16),
            pltpu.VMEM((8, full), f32),
        ),
        in_specs=[
            anywhere,
            pl.BlockSpec(memory_space=pltpu.SMEM),
            anywhere,
            anywhere,
            pl.BlockSpec(memory_space=pltpu.VMEM),
        ],
        out_specs=(pl.BlockSpec(memory_space=pltpu.VMEM),) * 3,
        scratch_shapes=scratch,
        compiler_params=pltpu.CompilerParams(
            collective_id=0, has_side_effects=True, vmem_limit_bytes=50 << 20
        ),
    )(capacity_blocks.reshape(local * per_block, edge, edge), capacity_rows.T, cover_self, cover_prev, scaling)


def solution(mesh):
    axes = ("var", "own", "sub")
    placed = (P(axes, None, None, None), P(axes, None), P(axes, None, None), P(axes, None, None), P(axes, None))
    return jax.shard_map(
        body,
        mesh=mesh,
        in_specs=placed,
        out_specs=(P(axes, None, None), P(axes, None, None), P(axes, None)),
        check_vma=False,
    )
```

```python
import functools

import jax
import jax.numpy as jnp
from jax import lax
from jax.experimental import pallas as pl
from jax.experimental.pallas import tpu as pltpu
from jax.sharding import PartitionSpec as P

MESH = pl.DeviceIdType.MESH
CAP = 8
TILE = 256
ORDER = (2, 1, 3, 0)
CHUNKS = (8, 16, 20, 20)
STARTS = (0, 8, 24, 44)
BATCHES = (
    ((0, 0), (0, 1), (0, 2), (0, 3), (1, 0), (2, 0), (3, 0)),
    ((1, 1), (1, 2), (1, 3), (2, 1), (3, 1)),
    ((2, 2), (2, 3), (3, 2)),
    ((3, 3),),
)
NT = (((1,), (1,)), ((), ()))


def kernel(sizes, cap_ref, rows_ref, self_ref, prev_ref, scal_ref, diag_ref, lower_ref, norm_ref, *scratch):
    local, per_block, edge = sizes
    group = local // 4
    scratch = list(scratch)
    raws = [scratch.pop(0) for _ in CHUNKS]
    scaled_raws = [scratch.pop(0) for _ in CHUNKS]
    core_send = [scratch.pop(0) for _ in range(4)]
    core_recv = [scratch.pop(0) for _ in range(4)]
    first_send = [scratch.pop(0) for _ in range(4)]
    first_recv = [scratch.pop(0) for _ in range(4)]
    second_send = [scratch.pop(0) for _ in range(4)]
    second_recv = [scratch.pop(0) for _ in range(4)]
    (acc, dsc, cself, cprev, bnd_block, bnd_scale, ysum, yrecv) = scratch[:8]
    (load_sem, cover_sem, bnd_send, bnd_recv, core_ssem, core_rsem,
     first_ssem, first_rsem, second_ssem, second_rsem, y_ssem, y_rsem) = scratch[8:]

    var, own, sub = lax.axis_index("var"), lax.axis_index("own"), lax.axis_index("sub")
    y, z, x = var // 4, var % 4, own
    here = (var * 4 + own) * 2 + sub

    def device(index):
        return (index // 8, (index // 2) % 4, index % 2)

    after, before = device((here + 1) % 128), device((here + 127) % 128)
    other = (var, own, 1 - sub)

    my_first, my_second = z * (1 - sub) + x * sub, x * (1 - sub) + z * sub

    def first_peer(d):
        return (y * 4 + (z + d * (1 - sub)) % 4, (x + d * sub) % 4, sub)

    def second_peer(d):
        return (y * 4 + (z + d * sub) % 4, (x + d * (1 - sub)) % 4, sub)

    def y_peer(t):
        return (((y + ORDER[t]) % 4) * 4 + z, x, sub)

    barrier = pltpu.get_barrier_semaphore()

    loads = []
    for c, size in enumerate(CHUNKS):
        copy = pltpu.make_async_copy(
            cap_ref.at[pl.ds(STARTS[c] * per_block, size * per_block)],
            raws[c].at[pl.ds(0, size * per_block)],
            load_sem.at[c],
        )
        loads.append(copy)
    cover_loads = [
        pltpu.make_async_copy(self_ref, cself.at[pl.ds(1, local)], cover_sem.at[0]),
        pltpu.make_async_copy(prev_ref, cprev, cover_sem.at[1]),
    ]
    for copy in loads:
        copy.start()

    for peer in (other, after, before):
        pl.semaphore_signal(barrier, inc=1, device_id=peer, device_id_type=MESH)
    for t in range(3):
        pl.semaphore_signal(barrier, inc=1, device_id=y_peer(t), device_id_type=MESH)

    for d in range(1, 4):
        pl.semaphore_signal(barrier, inc=1, device_id=first_peer(d), device_id_type=MESH)
        pl.semaphore_signal(barrier, inc=1, device_id=second_peer(d), device_id_type=MESH)

    blank = jnp.zeros((edge, edge), jnp.bfloat16)
    for c, size in enumerate(CHUNKS):
        raws[c][size * per_block] = blank
        scaled_raws[c][size * per_block] = blank
    dsc[pl.ds(8, local), :] = scal_ref[...].astype(jnp.float32)

    places = {}

    def place(c):
        for kk in range(CHUNKS[c]):
            named = [rows_ref[p, STARTS[c] + kk] for p in range(per_block)]
            for t in range(4):
                for h in range(2):
                    row = ((y + ORDER[t]) % 4) * 2 + h
                    at = jnp.int32(CHUNKS[c] * per_block)
                    for p in range(per_block):
                        at = jnp.where(named[p] == row, kk * per_block + p, at)
                    places[c, kk, t, h] = at

    def apply_scale(c):
        for kk in range(CHUNKS[c]):
            d = dsc[pl.ds(8 + STARTS[c] + kk, 1), :].astype(jnp.bfloat16)
            for p in range(per_block):
                scaled_raws[c][kk * per_block + p] = raws[c][kk * per_block + p] * d

    def operand(source, c, t):
        halves = [
            jnp.concatenate([source[c][places[c, kk, t, h]] for kk in range(CHUNKS[c])], axis=1)
            for h in range(2)
        ]
        return jnp.concatenate(halves, axis=0)

    def product(c, t, j):
        part = lax.dot_general(
            operand(scaled_raws, c, t), operand(raws, c, j), NT, preferred_element_type=jnp.float32
        )
        unit = (pl.ds(t * TILE, TILE), pl.ds(j * TILE, TILE))
        if c == 0:
            acc[unit] = part
        else:
            acc[unit] += part

    def unit_of(t, j):
        for c in range(len(CHUNKS)):
            product(c, t, j)

    core_copies = [
        pltpu.make_async_remote_copy(
            src_ref=core_send[b].at[1 - sub],
            dst_ref=core_recv[b],
            send_sem=core_ssem.at[b],
            recv_sem=core_rsem.at[b],
            device_id=other,
            device_id_type=MESH,
        )
        for b in range(4)
    ]

    def pack(b):
        for u, (t, j) in enumerate(BATCHES[b]):
            if t <= j:
                value = acc[pl.ds(t * TILE, TILE), pl.ds(j * TILE, TILE)]
            else:
                value = acc[pl.ds(j * TILE, TILE), pl.ds(t * TILE, TILE)].T
            value = value.reshape(16, 2, 8, TILE).astype(jnp.bfloat16)
            for c in range(2):
                core_send[b][c, :, pl.ds(u * 8, 8), :] = value[:, c]
        core_copies[b].start()

    first_copies = [
        [
            pltpu.make_async_remote_copy(
                src_ref=first_send[b].at[(my_first + d) % 4],
                dst_ref=first_recv[b].at[d],
                send_sem=first_ssem.at[b, d],
                recv_sem=first_rsem.at[b, d],
                device_id=first_peer(d),
                device_id_type=MESH,
            )
            for d in range(1, 4)
        ]
        for b in range(4)
    ]
    second_copies = [
        [
            pltpu.make_async_remote_copy(
                src_ref=second_send[b].at[(my_second + d) % 4],
                dst_ref=second_recv[b].at[d],
                send_sem=second_ssem.at[b, d],
                recv_sem=second_rsem.at[b, d],
                device_id=second_peer(d),
                device_id_type=MESH,
            )
            for d in range(1, 4)
        ]
        for b in range(4)
    ]

    def add_core(b):
        core_copies[b].wait_recv()
        for f in range(4):
            for g in range(4):
                at = (f * 4 + g) * (1 - sub) + (g * 4 + f) * sub
                first_send[b][f, g] = (
                    core_send[b][sub, at].astype(jnp.float32) + core_recv[b][at].astype(jnp.float32)
                ).astype(jnp.bfloat16)
        for copy in first_copies[b]:
            copy.start()

    def add_first(b):
        for copy in first_copies[b]:
            copy.wait_recv()
        total = first_send[b][my_first].astype(jnp.float32)
        for d in range(1, 4):
            total = total + first_recv[b][d].astype(jnp.float32)
        second_send[b][...] = total.astype(jnp.bfloat16)
        for copy in second_copies[b]:
            copy.start()

    y_copies = [
        pltpu.make_async_remote_copy(
            src_ref=ysum.at[t],
            dst_ref=yrecv.at[t],
            send_sem=y_ssem.at[t],
            recv_sem=y_rsem.at[t],
            device_id=y_peer(t),
            device_id_type=MESH,
        )
        for t in range(3)
    ]

    def add_second(b):
        for copy in second_copies[b]:
            copy.wait_recv()
        total = second_send[b][my_second].astype(jnp.float32)
        for d in range(1, 4):
            total = total + second_recv[b][d].astype(jnp.float32)
        for u, (t, j) in enumerate(BATCHES[b]):
            column = pl.multiple_of(((y + ORDER[j]) % 4) * TILE, TILE)
            ysum[t, :, pl.ds(column, TILE)] = total[u * 8 : (u + 1) * 8]
        if b < 3:
            y_copies[b].start()

    def cover(c):
        @pl.loop(c * group, (c + 1) * group, unroll=group)
        def _(k):
            d = dsc[pl.ds(k + 8, 1), :].astype(jnp.bfloat16)
            d_prev = dsc[pl.ds(k + 7, 1), :].astype(jnp.bfloat16)
            block, link = cself[k + 1], cprev[k]
            scaled, scaled_link = block * d, link * d_prev
            total = lax.dot_general(
                jnp.concatenate([scaled, scaled_link], axis=1),
                jnp.concatenate([block, link], axis=1),
                NT,
                preferred_element_type=jnp.float32,
            )
            diag_ref[k] = total.astype(jnp.bfloat16)
            lower_ref[k] = lax.dot_general(
                scaled_link, cself[k], NT, preferred_element_type=jnp.float32
            ).astype(jnp.bfloat16)

    for copy in cover_loads:
        copy.start()
    for c in range(len(CHUNKS)):
        place(c)
        loads[c].wait()
        apply_scale(c)
        for j in range(4):
            product(c, 0, j)

    pl.semaphore_wait(barrier, 12)
    boundary = [
        pltpu.make_async_remote_copy(
            src_ref=self_ref.at[local - 1],
            dst_ref=bnd_block,
            send_sem=bnd_send.at[0],
            recv_sem=bnd_recv.at[0],
            device_id=after,
            device_id_type=MESH,
        ),
        pltpu.make_async_remote_copy(
            src_ref=scal_ref.at[pl.ds(local - 16, 16)],
            dst_ref=bnd_scale,
            send_sem=bnd_send.at[1],
            recv_sem=bnd_recv.at[1],
            device_id=after,
            device_id_type=MESH,
        ),
    ]
    for copy in boundary:
        copy.start()
    pack(0)
    unit_of(1, 1)
    unit_of(1, 2)
    add_core(0)
    unit_of(1, 3)
    pack(1)
    unit_of(2, 2)
    unit_of(2, 3)
    add_core(1)
    pack(2)
    unit_of(3, 3)
    add_core(2)
    pack(3)

    for copy in cover_loads:
        copy.wait()
    for copy in boundary:
        copy.wait_recv()
    first = here == 0
    cself[0] = jnp.where(first, jnp.zeros_like(bnd_block), bnd_block[...])
    dsc[pl.ds(7, 1), :] = jnp.where(first, 0.0, bnd_scale[...].astype(jnp.float32)[15:16, :])

    cover(0)
    add_core(3)
    add_first(0)
    cover(1)
    add_first(1)
    add_second(0)
    cover(2)
    add_first(2)
    add_second(1)
    cover(3)
    add_first(3)
    add_second(2)
    add_second(3)
    total = ysum[3]
    for t in range(3):
        y_copies[t].wait_recv()
        total = total + yrecv[t]
    norm_ref[...] = total
    for copy in boundary + core_copies + y_copies:
        copy.wait_send()
    for b in range(4):
        for copy in first_copies[b] + second_copies[b]:
            copy.wait_send()


def write_out(*refs):
    held, outs, sem = refs[:3], refs[3:6], refs[6]
    copies = [pltpu.make_async_copy(held[i], outs[i], sem.at[i]) for i in range(3)]
    for copy in copies:
        copy.start()
    for copy in copies:
        copy.wait()


def body(capacity_blocks, capacity_rows, cover_self, cover_prev, scaling):
    local, per_block, edge, _ = capacity_blocks.shape
    full = CAP * edge
    bf16, f32 = jnp.bfloat16, jnp.float32
    counts = [len(batch) for batch in BATCHES]
    dma = pltpu.SemaphoreType.DMA
    scratch = [pltpu.VMEM((n * per_block + 1, edge, edge), bf16) for n in CHUNKS * 2]
    scratch += [pltpu.VMEM((2, 16, n * 8, TILE), bf16) for n in counts]
    scratch += [pltpu.VMEM((16, n * 8, TILE), bf16) for n in counts]
    scratch += [pltpu.VMEM((4, 4, n * 8, TILE), bf16) for n in counts * 2]
    scratch += [pltpu.VMEM((4, n * 8, TILE), bf16) for n in counts * 2]
    scratch += [
        pltpu.VMEM((full, full), f32),
        pltpu.VMEM((local + 8, edge), f32),
        pltpu.VMEM((local + 1, edge, edge), bf16),
        pltpu.VMEM((local, edge, edge), bf16),
        pltpu.VMEM((edge, edge), bf16),
        pltpu.VMEM((16, edge), bf16),
        pltpu.VMEM((4, 8, full), f32),
        pltpu.VMEM((3, 8, full), f32),
    ]
    scratch += [
        dma((len(CHUNKS),)), dma((2,)), dma((2,)), dma((2,)),
        dma((4,)), dma((4,)), dma((4, 4)), dma((4, 4)), dma((4, 4)), dma((4, 4)), dma((3,)), dma((3,)),
    ]
    anywhere = pl.BlockSpec(memory_space=pl.ANY)
    held = pl.pallas_call(
        functools.partial(kernel, (local, per_block, edge)),
        out_shape=(
            pltpu.VMEM((local, edge, edge), bf16),
            pltpu.VMEM((local, edge, edge), bf16),
            pltpu.VMEM((8, full), f32),
        ),
        in_specs=[
            anywhere,
            pl.BlockSpec(memory_space=pltpu.SMEM),
            anywhere,
            anywhere,
            pl.BlockSpec(memory_space=pltpu.VMEM),
        ],
        out_specs=(pl.BlockSpec(memory_space=pltpu.VMEM),) * 3,
        scratch_shapes=scratch,
        compiler_params=pltpu.CompilerParams(
            collective_id=0, has_side_effects=True, vmem_limit_bytes=50 << 20
        ),
    )(capacity_blocks.reshape(local * per_block, edge, edge), capacity_rows.T, cover_self, cover_prev, scaling)
    return pl.pallas_call(
        write_out,
        out_shape=tuple(jax.ShapeDtypeStruct(value.shape, value.dtype) for value in held),
        in_specs=[pl.BlockSpec(memory_space=pltpu.VMEM)] * 3,
        out_specs=(anywhere,) * 3,
        scratch_shapes=[dma((3,))],
        compiler_params=pltpu.CompilerParams(vmem_limit_bytes=1 << 20),
    )(*held)


def solution(mesh):
    axes = ("var", "own", "sub")
    placed = (P(axes, None, None, None), P(axes, None), P(axes, None, None), P(axes, None, None), P(axes, None))
    return jax.shard_map(
        body,
        mesh=mesh,
        in_specs=placed,
        out_specs=(P(axes, None, None), P(axes, None, None), P(axes, None)),
        check_vma=False,
    )
```

```python
import functools

import jax
import jax.numpy as jnp
from jax import lax
from jax.experimental import pallas as pl
from jax.experimental.pallas import tpu as pltpu
from jax.sharding import PartitionSpec as P

MESH = pl.DeviceIdType.MESH
CAP = 8
TILE = 256
ORDER = (2, 1, 3, 0)
CHUNKS = (8, 16, 20, 20)
STARTS = (0, 8, 24, 44)
BATCHES = (
    ((0, 0), (0, 1), (0, 2), (0, 3), (1, 0), (2, 0), (3, 0)),
    ((1, 1), (1, 2), (1, 3), (2, 1), (3, 1)),
    ((2, 2), (2, 3), (3, 2)),
    ((3, 3),),
)
NT = (((1,), (1,)), ((), ()))


def kernel(sizes, cap_ref, rows_ref, self_ref, prev_ref, scal_ref, diag_ref, lower_ref, norm_ref, *scratch):
    local, per_block, edge = sizes
    group = local // 4
    scratch = list(scratch)
    raws = [scratch.pop(0) for _ in CHUNKS]
    scaled_raws = [scratch.pop(0) for _ in CHUNKS]
    core_send = [scratch.pop(0) for _ in range(4)]
    core_recv = [scratch.pop(0) for _ in range(4)]
    first_send = [scratch.pop(0) for _ in range(4)]
    first_recv = [scratch.pop(0) for _ in range(4)]
    second_send = [scratch.pop(0) for _ in range(4)]
    second_recv = [scratch.pop(0) for _ in range(4)]
    (acc, dsc, cself, cprev, bnd_block, bnd_scale, ysum, yrecv) = scratch[:8]
    (load_sem, cover_sem, bnd_send, bnd_recv, core_ssem, core_rsem,
     first_ssem, first_rsem, second_ssem, second_rsem, y_ssem, y_rsem) = scratch[8:]

    var, own, sub = lax.axis_index("var"), lax.axis_index("own"), lax.axis_index("sub")
    y, z, x = var // 4, var % 4, own
    here = (var * 4 + own) * 2 + sub

    def device(index):
        return (index // 8, (index // 2) % 4, index % 2)

    after, before = device((here + 1) % 128), device((here + 127) % 128)
    other = (var, own, 1 - sub)

    my_first, my_second = z * (1 - sub) + x * sub, x * (1 - sub) + z * sub

    def first_peer(d):
        return (y * 4 + (z + d * (1 - sub)) % 4, (x + d * sub) % 4, sub)

    def second_peer(d):
        return (y * 4 + (z + d * sub) % 4, (x + d * (1 - sub)) % 4, sub)

    def y_peer(t):
        return (((y + ORDER[t]) % 4) * 4 + z, x, sub)

    barrier = pltpu.get_barrier_semaphore()

    loads = []
    for c, size in enumerate(CHUNKS):
        copy = pltpu.make_async_copy(
            cap_ref.at[pl.ds(STARTS[c] * per_block, size * per_block)],
            raws[c].at[pl.ds(0, size * per_block)],
            load_sem.at[c],
        )
        loads.append(copy)
    cover_loads = [
        pltpu.make_async_copy(self_ref, cself.at[pl.ds(1, local)], cover_sem.at[0]),
        pltpu.make_async_copy(prev_ref, cprev, cover_sem.at[1]),
    ]
    for copy in loads:
        copy.start()

    for peer in (other, after, before):
        pl.semaphore_signal(barrier, inc=1, device_id=peer, device_id_type=MESH)
    for t in range(3):
        pl.semaphore_signal(barrier, inc=1, device_id=y_peer(t), device_id_type=MESH)

    for d in range(1, 4):
        pl.semaphore_signal(barrier, inc=1, device_id=first_peer(d), device_id_type=MESH)
        pl.semaphore_signal(barrier, inc=1, device_id=second_peer(d), device_id_type=MESH)

    blank = jnp.zeros((edge, edge), jnp.bfloat16)
    for c, size in enumerate(CHUNKS):
        raws[c][size * per_block] = blank
        scaled_raws[c][size * per_block] = blank
    dsc[pl.ds(8, local), :] = scal_ref[...].astype(jnp.float32)

    places = {}

    def place(c):
        for kk in range(CHUNKS[c]):
            named = [rows_ref[p, STARTS[c] + kk] for p in range(per_block)]
            for t in range(4):
                for h in range(2):
                    row = ((y + ORDER[t]) % 4) * 2 + h
                    at = jnp.int32(CHUNKS[c] * per_block)
                    for p in range(per_block):
                        at = jnp.where(named[p] == row, kk * per_block + p, at)
                    places[c, kk, t, h] = at

    def apply_scale(c):
        for kk in range(CHUNKS[c]):
            d = dsc[pl.ds(8 + STARTS[c] + kk, 1), :].astype(jnp.bfloat16)
            for p in range(per_block):
                scaled_raws[c][kk * per_block + p] = raws[c][kk * per_block + p] * d

    def operand(source, c, t):
        halves = [
            jnp.concatenate([source[c][places[c, kk, t, h]] for kk in range(CHUNKS[c])], axis=1)
            for h in range(2)
        ]
        return jnp.concatenate(halves, axis=0)

    def product(c, t, j):
        part = lax.dot_general(
            operand(scaled_raws, c, t), operand(raws, c, j), NT, preferred_element_type=jnp.float32
        )
        unit = (pl.ds(t * TILE, TILE), pl.ds(j * TILE, TILE))
        if c == 0:
            acc[unit] = part
        else:
            acc[unit] += part

    def unit_of(t, j):
        for c in range(len(CHUNKS)):
            product(c, t, j)

    core_copies = [
        pltpu.make_async_remote_copy(
            src_ref=core_send[b].at[1 - sub],
            dst_ref=core_recv[b],
            send_sem=core_ssem.at[b],
            recv_sem=core_rsem.at[b],
            device_id=other,
            device_id_type=MESH,
        )
        for b in range(4)
    ]

    def pack(b):
        for u, (t, j) in enumerate(BATCHES[b]):
            if t <= j:
                value = acc[pl.ds(t * TILE, TILE), pl.ds(j * TILE, TILE)]
            else:
                value = acc[pl.ds(j * TILE, TILE), pl.ds(t * TILE, TILE)].T
            value = value.reshape(16, 2, 8, TILE).astype(jnp.bfloat16)
            for c in range(2):
                core_send[b][c, :, pl.ds(u * 8, 8), :] = value[:, c]
        core_copies[b].start()

    first_copies = [
        [
            pltpu.make_async_remote_copy(
                src_ref=first_send[b].at[(my_first + d) % 4],
                dst_ref=first_recv[b].at[d],
                send_sem=first_ssem.at[b, d],
                recv_sem=first_rsem.at[b, d],
                device_id=first_peer(d),
                device_id_type=MESH,
            )
            for d in range(1, 4)
        ]
        for b in range(4)
    ]
    second_copies = [
        [
            pltpu.make_async_remote_copy(
                src_ref=second_send[b].at[(my_second + d) % 4],
                dst_ref=second_recv[b].at[d],
                send_sem=second_ssem.at[b, d],
                recv_sem=second_rsem.at[b, d],
                device_id=second_peer(d),
                device_id_type=MESH,
            )
            for d in range(1, 4)
        ]
        for b in range(4)
    ]

    def add_core(b):
        core_copies[b].wait_recv()
        for f in range(4):
            for g in range(4):
                at = (f * 4 + g) * (1 - sub) + (g * 4 + f) * sub
                first_send[b][f, g] = (
                    core_send[b][sub, at].astype(jnp.float32) + core_recv[b][at].astype(jnp.float32)
                ).astype(jnp.bfloat16)
        for copy in first_copies[b]:
            copy.start()

    def add_first(b):
        for copy in first_copies[b]:
            copy.wait_recv()
        total = first_send[b][my_first].astype(jnp.float32)
        for d in range(1, 4):
            total = total + first_recv[b][d].astype(jnp.float32)
        second_send[b][...] = total.astype(jnp.bfloat16)
        for copy in second_copies[b]:
            copy.start()

    y_copies = [
        pltpu.make_async_remote_copy(
            src_ref=ysum.at[t],
            dst_ref=yrecv.at[t],
            send_sem=y_ssem.at[t],
            recv_sem=y_rsem.at[t],
            device_id=y_peer(t),
            device_id_type=MESH,
        )
        for t in range(3)
    ]

    def add_second(b):
        for copy in second_copies[b]:
            copy.wait_recv()
        total = second_send[b][my_second].astype(jnp.float32)
        for d in range(1, 4):
            total = total + second_recv[b][d].astype(jnp.float32)
        for u, (t, j) in enumerate(BATCHES[b]):
            column = pl.multiple_of(((y + ORDER[j]) % 4) * TILE, TILE)
            ysum[t, :, pl.ds(column, TILE)] = total[u * 8 : (u + 1) * 8]
        if b < 3:
            y_copies[b].start()

    def cover(c):
        @pl.loop(c * group, (c + 1) * group, unroll=group)
        def _(k):
            d = dsc[pl.ds(k + 8, 1), :].astype(jnp.bfloat16)
            d_prev = dsc[pl.ds(k + 7, 1), :].astype(jnp.bfloat16)
            block, link = cself[k + 1], cprev[k]
            scaled, scaled_link = block * d, link * d_prev
            total = lax.dot_general(
                jnp.concatenate([scaled, scaled_link], axis=1),
                jnp.concatenate([block, link], axis=1),
                NT,
                preferred_element_type=jnp.float32,
            )
            diag_ref[k] = total.astype(jnp.bfloat16)
            lower_ref[k] = lax.dot_general(
                scaled_link, cself[k], NT, preferred_element_type=jnp.float32
            ).astype(jnp.bfloat16)

    for copy in cover_loads:
        copy.start()
    for c in range(len(CHUNKS)):
        place(c)
        loads[c].wait()
        apply_scale(c)
        for j in range(4):
            product(c, 0, j)

    pl.semaphore_wait(barrier, 12)
    boundary = [
        pltpu.make_async_remote_copy(
            src_ref=self_ref.at[local - 1],
            dst_ref=bnd_block,
            send_sem=bnd_send.at[0],
            recv_sem=bnd_recv.at[0],
            device_id=after,
            device_id_type=MESH,
        ),
        pltpu.make_async_remote_copy(
            src_ref=scal_ref.at[pl.ds(local - 16, 16)],
            dst_ref=bnd_scale,
            send_sem=bnd_send.at[1],
            recv_sem=bnd_recv.at[1],
            device_id=after,
            device_id_type=MESH,
        ),
    ]
    for copy in boundary:
        copy.start()
    pack(0)
    unit_of(1, 1)
    unit_of(1, 2)
    add_core(0)
    unit_of(1, 3)
    pack(1)
    unit_of(2, 2)
    unit_of(2, 3)
    add_core(1)
    pack(2)
    unit_of(3, 3)
    add_core(2)
    pack(3)

    for copy in cover_loads:
        copy.wait()
    for copy in boundary:
        copy.wait_recv()
    first = here == 0
    cself[0] = jnp.where(first, jnp.zeros_like(bnd_block), bnd_block[...])
    dsc[pl.ds(7, 1), :] = jnp.where(first, 0.0, bnd_scale[...].astype(jnp.float32)[15:16, :])

    cover(0)
    add_core(3)
    add_first(0)
    add_first(1)
    cover(1)
    add_second(0)
    add_first(2)
    add_first(3)
    cover(2)
    add_second(1)
    add_second(2)
    cover(3)
    add_second(3)
    total = ysum[3]
    for t in range(3):
        y_copies[t].wait_recv()
        total = total + yrecv[t]
    norm_ref[...] = total
    for copy in boundary + core_copies + y_copies:
        copy.wait_send()
    for b in range(4):
        for copy in first_copies[b] + second_copies[b]:
            copy.wait_send()


def write_out(*refs):
    held, outs, sem = refs[:3], refs[3:6], refs[6]
    copies = [pltpu.make_async_copy(held[i], outs[i], sem.at[i]) for i in range(3)]
    for copy in copies:
        copy.start()
    for copy in copies:
        copy.wait()


def body(capacity_blocks, capacity_rows, cover_self, cover_prev, scaling):
    local, per_block, edge, _ = capacity_blocks.shape
    full = CAP * edge
    bf16, f32 = jnp.bfloat16, jnp.float32
    counts = [len(batch) for batch in BATCHES]
    dma = pltpu.SemaphoreType.DMA
    scratch = [pltpu.VMEM((n * per_block + 1, edge, edge), bf16) for n in CHUNKS * 2]
    scratch += [pltpu.VMEM((2, 16, n * 8, TILE), bf16) for n in counts]
    scratch += [pltpu.VMEM((16, n * 8, TILE), bf16) for n in counts]
    scratch += [pltpu.VMEM((4, 4, n * 8, TILE), bf16) for n in counts * 2]
    scratch += [pltpu.VMEM((4, n * 8, TILE), bf16) for n in counts * 2]
    scratch += [
        pltpu.VMEM((full, full), f32),
        pltpu.VMEM((local + 8, edge), f32),
        pltpu.VMEM((local + 1, edge, edge), bf16),
        pltpu.VMEM((local, edge, edge), bf16),
        pltpu.VMEM((edge, edge), bf16),
        pltpu.VMEM((16, edge), bf16),
        pltpu.VMEM((4, 8, full), f32),
        pltpu.VMEM((3, 8, full), f32),
    ]
    scratch += [
        dma((len(CHUNKS),)), dma((2,)), dma((2,)), dma((2,)),
        dma((4,)), dma((4,)), dma((4, 4)), dma((4, 4)), dma((4, 4)), dma((4, 4)), dma((3,)), dma((3,)),
    ]
    anywhere = pl.BlockSpec(memory_space=pl.ANY)
    held = pl.pallas_call(
        functools.partial(kernel, (local, per_block, edge)),
        out_shape=(
            pltpu.VMEM((local, edge, edge), bf16),
            pltpu.VMEM((local, edge, edge), bf16),
            pltpu.VMEM((8, full), f32),
        ),
        in_specs=[
            anywhere,
            pl.BlockSpec(memory_space=pltpu.SMEM),
            anywhere,
            anywhere,
            pl.BlockSpec(memory_space=pltpu.VMEM),
        ],
        out_specs=(pl.BlockSpec(memory_space=pltpu.VMEM),) * 3,
        scratch_shapes=scratch,
        compiler_params=pltpu.CompilerParams(
            collective_id=0, has_side_effects=True, vmem_limit_bytes=50 << 20
        ),
    )(capacity_blocks.reshape(local * per_block, edge, edge), capacity_rows.T, cover_self, cover_prev, scaling)
    return pl.pallas_call(
        write_out,
        out_shape=tuple(jax.ShapeDtypeStruct(value.shape, value.dtype) for value in held),
        in_specs=[pl.BlockSpec(memory_space=pltpu.VMEM)] * 3,
        out_specs=(anywhere,) * 3,
        scratch_shapes=[dma((3,))],
        compiler_params=pltpu.CompilerParams(vmem_limit_bytes=1 << 20),
    )(*held)


def solution(mesh):
    axes = ("var", "own", "sub")
    placed = (P(axes, None, None, None), P(axes, None), P(axes, None, None), P(axes, None, None), P(axes, None))
    return jax.shard_map(
        body,
        mesh=mesh,
        in_specs=placed,
        out_specs=(P(axes, None, None), P(axes, None, None), P(axes, None)),
        check_vma=False,
    )
```
